32 devices in a mesh: bpm: 4 (over y, x), cor: 8 (over z, core).
Axes of the slice: x: 2, y: 2, z: 4, core: 2. Of those that a mesh axis runs over, the one named last changes fastest.
Arguments:
- quad_bpm: bfloat16 [6144, 2048], P('cor', 'bpm'), may hold values from -0.078125 to 0.078125
- cor_quad: bfloat16 [6144, 6144], P('cor', 'bpm'), may hold values from -0.875 to 0.875
- step: float32 [6144], P(('bpm', 'cor')), may hold values from -6 to 6
- quad_order: int32 [6144], replicated, may hold values from 0 to 6143, each once
- bpm_mask: int32 [2048], P('bpm'), may hold values 0 or 1
- bpm_noise: float32 [2048], P('bpm'), may hold values from 0.5 to 2
Outputs:
- product: float32 [6144], P(('bpm', 'cor'))
The draws below stay inside these ranges and needn't reach their ends.
Inputs may be any that keep to these rules, and one draw needn't show every extreme that they name: `quad_order`: each parameter drives exactly one quadrupole.
All inputs are finite; a program needn't handle non-finite values. No bound on the sum of `bpm_mask` on one device may be relied on, other than what follows from the above.
Results may differ from the reference program's by a relative error of at most 0.00035.
Values may be sent and summed in bfloat16 or wider, within the bound.
No kernel may reach another device: no remote copies, remote signals or barrier semaphores. Data moves between devices by JAX's collectives and lax.ppermute only.
A program may use at most 64 MiB of HBM per device.

```python
import math
import jax
import jax.numpy as jnp
from jax import lax

NQ = 6144
NC = 6144
NB = 2048


def plant(values, own_key, smallest, high):
    index_at = [jax.random.randint(jax.random.fold_in(own_key, axis), (), 0, length) for axis, length in enumerate(values.shape)]
    widest = values.shape.index(max(values.shape))
    neighbour = index_at[:widest] + [(index_at[widest] + 1) % values.shape[widest]] + index_at[widest + 1:]
    return values.at[tuple(index_at)].set(smallest).at[tuple(neighbour)].set(high)


def level_of(stream_key, dims, shards, smallest, high):
    def one(dim, shards_of):
        draws = jax.random.uniform(jax.random.fold_in(jax.random.fold_in(stream_key, 6), dim), (shards_of,), jnp.float32, smallest / len(shards), high / len(shards))
        return jnp.repeat(jnp.exp(draws), dims[dim] // shards_of).reshape((-1,) + (1,) * (len(dims) - dim - 1))

    level = one(*shards[0])
    for cut in shards[1:]:
        level = level * one(*cut)
    return level


def noise(key, extent, width, limit, pieces=(), held_as=jnp.bfloat16):
    result = jax.random.normal(key, extent, jnp.float32) * width
    if len(pieces) > 0:
        result = level_of(key, extent, pieces, -0.22, 0.18) * result
    return jnp.clip(result, min=-limit, max=limit).astype(held_as)


def setup_inputs(seed: int = 0) -> dict:
    keys = jax.random.split(jax.random.key(seed), 7)
    quad_bpm = noise(keys[0], (NQ, NB), NQ ** -0.5, 0.078125, ((0, 8), (1, 4)))
    cor_quad = noise(keys[1], (NC, NQ), (NB ** 0.5) ** -0.5, 0.875, ((0, 8), (1, 4)))
    step = noise(keys[2], (NQ,), 1.0, 6.0, ((0, 32),), jnp.float32)
    quad_order = jax.random.permutation(keys[3], NQ).astype(jnp.int32)
    bpm_mask = plant((jax.random.randint(keys[4], (NB,), 0, 8) < 7).astype(jnp.int32), jax.random.fold_in(keys[4], 1), 0, 1)
    bpm_noise = jnp.clip(jnp.exp(math.log(2.0) - 1.3862944 * jax.random.uniform(keys[5], (NB,), jnp.float32) ** level_of(keys[5], (NB,), ((0, 4),), -0.2, 0.2)), 0.5, 2.0)
    return {"quad_bpm": quad_bpm, "cor_quad": cor_quad, "step": step, "quad_order": quad_order, "bpm_mask": bpm_mask, "bpm_noise": bpm_noise}


def reference(quad_bpm, cor_quad, step, quad_order, bpm_mask, bpm_noise):
    u_vec = step[quad_order]
    scaled = (u_vec[None, :] * cor_quad.astype(jnp.float32)).astype(jnp.bfloat16)
    response = jnp.dot(scaled, quad_bpm, preferred_element_type=jnp.float32)
    weight = bpm_mask.astype(jnp.float32) / (bpm_noise * bpm_noise)
    weighted = (weight[None, :] * response).astype(jnp.bfloat16)
    back = lax.dot_general(cor_quad, weighted, (((0,), (0,)), ((), ())), preferred_element_type=jnp.float32)
    d_vec = jnp.sum(quad_bpm.astype(jnp.float32) * back, axis=1)
    return jnp.zeros((NQ,), jnp.float32).at[quad_order].set(d_vec)
```

```python
import functools

import jax
import jax.numpy as jnp
from jax import lax
from jax.experimental import pallas as pl
from jax.experimental.pallas import tpu as pltpu
from jax.sharding import PartitionSpec as P

AXES = ("bpm", "cor")
LANES = 128
CHUNKS = 3


def chunk_kernel(pieces, where_ref, *refs):
    a_refs, (b_ref, u_ref, w_ref, d_ref) = refs[:pieces], refs[pieces:]
    response = None
    for j in range(pieces):
        at = where_ref[j]
        scaled = (u_ref[at] * a_refs[j][...].astype(jnp.float32)).astype(jnp.bfloat16)
        term = jnp.dot(scaled, b_ref[at], preferred_element_type=jnp.float32)
        response = term if response is None else response + term
    weighted = (w_ref[...] * response).astype(jnp.bfloat16)
    for j in range(pieces):
        at = where_ref[j]
        spread = lax.dot_general(
            weighted, b_ref[at], (((1,), (1,)), ((), ())), preferred_element_type=jnp.float32
        )
        d_ref[at] = jnp.sum(a_refs[j][...].astype(jnp.float32) * spread, axis=0, keepdims=True)


def apply_chunk(a_pieces, where, b_all, u_all, weight):
    pieces = len(a_pieces)
    rows, width = a_pieces[0].shape
    cols = weight.shape[1]
    vmem = pl.BlockSpec(memory_space=pltpu.VMEM)
    return pl.pallas_call(
        functools.partial(chunk_kernel, pieces),
        out_shape=jax.ShapeDtypeStruct((pieces, 1, width), jnp.float32),
        in_specs=[pl.BlockSpec(memory_space=pltpu.SMEM)] + [vmem] * (pieces + 3),
        out_specs=vmem,
        compiler_params=pltpu.CompilerParams(vmem_limit_bytes=48 << 20),
        cost_estimate=pl.CostEstimate(
            flops=4 * rows * pieces * width * cols,
            bytes_accessed=2 * pieces * width * (rows + cols),
            transcendentals=0,
        ),
    )(where, *a_pieces, b_all, u_all, weight)


def face_perms(nb, nc):
    def pairs(bit):
        return [(p * nc + c, (p ^ bit) * nc + c) for p in range(nb) for c in range(nc)]
    return pairs(1), pairs(2)


def line_perms(nb, nc):
    up = [(p * nc + c, p * nc + c + 2) for p in range(nb) for c in range(nc - 2)]
    down = [(t, s) for s, t in up]
    core = [(p * nc + c, p * nc + (c ^ 1)) for p in range(nb) for c in range(nc)]
    return up, down, core


def gather_lines(block, nb, nc):
    up_perm, down_perm, core_perm = line_perms(nb, nc)
    n_line = nc // 2
    c = lax.axis_index("cor")
    place, core = c // 2, c % 2
    up, down = [None], [None]
    for _ in range(n_line - 1):
        up.append(lax.ppermute(block if up[-1] is None else up[-1], AXES, up_perm))
        down.append(lax.ppermute(block if down[-1] is None else down[-1], AXES, down_perm))
    rows, cols = block.shape
    out = jnp.zeros((n_line * 2 * rows, cols), block.dtype)
    for r in range(n_line):
        mine = block if r == 0 else up[r] + down[n_line - r]
        other = lax.ppermute(mine, AXES, core_perm)
        at = lax.rem(place - r + n_line, n_line) * 2
        out = lax.dynamic_update_slice(out, mine, ((at + core) * rows, 0))
        out = lax.dynamic_update_slice(out, other, ((at + 1 - core) * rows, 0))
    return out


def on_device(nb, nc, quad_bpm, cor_quad, step, quad_order, bpm_mask, bpm_noise):
    n_all = nb * nc
    share = step.shape[0]
    n_quads = quad_order.shape[0]
    rows, width = cor_quad.shape
    p = lax.axis_index("bpm")
    if nb == 4 and nc % 2 == 0 and rows % (2 * CHUNKS) == 0:
        low, high = face_perms(nb, nc)
        r = rows // CHUNKS
        own = [cor_quad[i * r:(i + 1) * r] for i in range(CHUNKS)]
        from_low = [lax.ppermute(a, AXES, low) for a in own]
        from_high = [lax.ppermute(a, AXES, high) for a in own]
        across = [
            jnp.concatenate(
                [lax.ppermute(a[: r // 2], AXES, high), lax.ppermute(b[r // 2:], AXES, low)], axis=0
            )
            for a, b in zip(from_low, from_high)
        ]
        chunks = list(zip(own, from_low, from_high, across))
        where = jnp.bitwise_xor(p, jnp.arange(nb, dtype=jnp.int32))
        b_all = gather_lines(quad_bpm, nb, nc)
    else:
        whole = lax.all_gather(cor_quad, "bpm", axis=0, tiled=False)
        chunks = [tuple(whole[j] for j in range(nb))]
        where = jnp.arange(nb, dtype=jnp.int32)
        b_all = lax.all_gather(quad_bpm, "cor", axis=0, tiled=True)
    whole_step = lax.all_to_all(
        jnp.broadcast_to(step, (n_all, share)), AXES, 0, 0, tiled=True
    ).reshape(n_quads // LANES, LANES)
    high_hot = (quad_order[None, :] // LANES == jnp.arange(n_quads // LANES, dtype=jnp.int32)[:, None]).astype(jnp.float32)
    low_hot = (quad_order[None, :] % LANES == jnp.arange(LANES, dtype=jnp.int32)[:, None]).astype(jnp.float32)
    spread = lax.dot_general(
        whole_step, high_hot, (((0,), (0,)), ((), ())), precision=lax.Precision.HIGHEST
    )
    u_all = jnp.sum(spread * low_hot, axis=0).reshape(nb, 1, width)
    weight = (bpm_mask.astype(jnp.float32) / (bpm_noise * bpm_noise))[None, :]
    b_all = b_all.reshape(nb, width, weight.shape[1])
    d_vec = sum(apply_chunk(c, where, b_all, u_all, weight) for c in chunks).reshape(1, n_quads)
    placed = lax.dot_general(
        high_hot * d_vec, low_hot, (((1,), (1,)), ((), ())), precision=lax.Precision.HIGHEST
    ).reshape(n_all, share)
    parts = lax.all_to_all(placed, AXES, 0, 0, tiled=True)
    return jnp.sum(parts, axis=0)


def solution(mesh):
    placed = (P("cor", "bpm"), P("cor", "bpm"), P(("bpm", "cor")), P(), P("bpm"), P("bpm"))
    body = functools.partial(on_device, mesh.shape["bpm"], mesh.shape["cor"])
    return jax.shard_map(
        body, mesh=mesh, in_specs=placed, out_specs=P(("bpm", "cor")), check_vma=False
    )
```
